32 devices in a mesh: section: 2 (over x), mesh: 16 (over z, y, core).
Axes of the slice: x: 2, y: 2, z: 4, core: 2. Of those that a mesh axis runs over, the one named last changes fastest.
Arguments:
- video_tokens: bfloat16 [2, 128, 6144], P(None, 'mesh'), may hold values from -6 to 6
- norm_gain: float32 [2, 6144], P('section'), may hold values from 0.5 to 2
- qkv_weight: bfloat16 [2, 6144, 18432], P('section', None, 'mesh'), may hold values from -0.078125 to 0.078125
- out_weight: bfloat16 [2, 6144, 6144], P('section', 'mesh'), may hold values from -0.078125 to 0.078125
Outputs:
- final_tokens: float32 [2, 128, 6144], P(None, 'mesh', 'section')
The draws below stay inside these ranges and needn't reach their ends.
All inputs are finite; a program needn't handle non-finite values.
Results may differ from the reference program's by a relative error of at most 0.023.
Values may be sent and summed in bfloat16 or wider, within the bound.
No kernel may reach another device: no remote copies, remote signals or barrier semaphores. Data moves between devices by JAX's collectives and lax.ppermute only.
A program may use at most 64 MiB of HBM per device.

```python
import jax
import jax.numpy as jnp
from jax import lax

D = 6144
HEADS = 64
HEAD_DIM = 96
PATCHES = 64
FRAMES = 2
MICRO = 2
SECTIONS = 2
TOKENS = 128


def draw_norm_gain(key, part):
    return jax.random.uniform(key, (SECTIONS, D), jnp.float32, 0.6, 1.6)


def block_levels(rng, dims, cuts, least, high):
    gain = 1.0
    for dim, shards_of in cuts:
        steps = jax.random.uniform(jax.random.fold_in(jax.random.fold_in(rng, 6), dim), (shards_of,), jnp.float32, least / len(cuts), high / len(cuts))
        gain = gain * jnp.repeat(jnp.exp(steps), dims[dim] // shards_of).reshape((-1,) + (1,) * (len(dims) - 1 - dim))
    return gain


def scatter_about(stream_key, shape, deviation, bound, split=(), held_as=jnp.bfloat16):
    result = jax.random.normal(stream_key, shape, jnp.float32) * deviation
    if len(split) > 0:
        result = block_levels(stream_key, shape, split, -0.22, 0.18) * result
    return jnp.clip(result, min=-bound, max=bound).astype(held_as)


def setup_inputs(seed: int = 0) -> dict:
    key_list = jax.random.split(jax.random.key(seed), 5)
    video_tokens = scatter_about(key_list[0], (MICRO, TOKENS, D), 1.0, 6.0, ((1, 16),))
    norm_gain = draw_norm_gain(jax.random.fold_in(key_list[4], 71), 0)
    qkv_weight = scatter_about(key_list[2], (SECTIONS, D, 3 * HEADS * HEAD_DIM), D ** -0.5, 0.078125, ((0, 2), (2, 16)))
    out_weight = scatter_about(key_list[3], (SECTIONS, HEADS * HEAD_DIM, D), (HEADS * HEAD_DIM) ** -0.5, 0.078125, ((0, 2), (1, 16)))
    return {"video_tokens": video_tokens, "norm_gain": norm_gain, "qkv_weight": qkv_weight, "out_weight": out_weight}


epsilon = 1e-06

def token_masks():
    row_ids = jnp.arange(FRAMES * PATCHES, dtype=jnp.int32)
    same_frame = row_ids[:, None] // PATCHES == row_ids[None, :] // PATCHES
    same_patch = row_ids[:, None] % PATCHES == row_ids[None, :] % PATCHES
    return (same_frame, same_patch)

def attention_layer(residual, gain_row, packed_weight, out_rows, attend_mask):
    wide = residual.astype(jnp.float32)
    mean_square = lax.optimization_barrier(jnp.mean(wide * wide, axis=-1, keepdims=True))
    normed = (wide * lax.rsqrt(mean_square + epsilon) * gain_row[None, :].astype(jnp.float32)).astype(jnp.bfloat16)
    packed = jnp.dot(normed, packed_weight, preferred_element_type=jnp.float32).astype(jnp.bfloat16)
    tokens = normed.shape[0]
    packed = packed.reshape(tokens, HEADS, 3, HEAD_DIM)
    queries = packed[:, :, 0].astype(jnp.float32)
    key_rows = packed[:, :, 1].astype(jnp.float32)
    value_rows = packed[:, :, 2].astype(jnp.float32)
    scores = jnp.einsum('thd,shd->hts', queries, key_rows) * HEAD_DIM ** (-0.5)
    scores = jnp.where(attend_mask[None], scores, -1e+30)
    weights = jax.nn.softmax(scores, axis=-1).astype(jnp.bfloat16)
    attended = jnp.einsum('hts,shd->thd', weights.astype(jnp.float32), value_rows)
    attended = attended.astype(jnp.bfloat16).reshape(tokens, HEADS * HEAD_DIM)
    projected = jnp.dot(attended, out_rows, preferred_element_type=jnp.float32)
    return wide + projected

def reference(video_tokens, norm_gain, qkv_weight, out_weight):
    same_frame, same_patch = token_masks()
    results = []
    for micro in range(MICRO):
        residual = video_tokens[micro].astype(jnp.float32)
        for layer in range(SECTIONS):
            attend_mask = same_frame if layer % 2 == 0 else same_patch
            residual = attention_layer(residual, norm_gain[layer], qkv_weight[layer], out_weight[layer], attend_mask)
        results.append(residual)
    return jnp.stack(results)
```

```python
import jax
import jax.numpy as jnp
from jax import lax
from jax.sharding import PartitionSpec as P

HEAD_DIM = 96
PATCHES = 64
CORES = 2

epsilon = 1e-06


def grid_of(devices):
    chips = devices // CORES
    wide = 1
    while wide * wide * 4 <= chips:
        wide *= 2
    return chips // wide, wide


def shifted(block, up, across, over):
    devices = lax.axis_size("mesh")
    tall, wide = grid_of(devices)
    route = []
    for i in range(devices):
        z, y, c = i // (CORES * wide), i // CORES % wide, i % CORES
        j = (((z + up) % tall) * wide + (y + across) % wide) * CORES + (c + over) % CORES
        route.append((i, j))
    return lax.ppermute(block, "mesh", route)


def passed_along(block, axis, distance):
    devices = range(lax.axis_size(axis))
    route = [(i - distance, i) for i in devices if i - distance in devices]
    return lax.ppermute(block, axis, route)


def gathered(block):
    tall, wide = grid_of(lax.axis_size("mesh"))
    column = {0: block}
    order = sorted(range(1, tall), key=lambda s: -min(s, tall - s))
    for s in order:
        column[s] = shifted(block, s, 0, 0)
    pieces = {(0, t): shifted(block, 0, t, 0) if t else block for t in range(wide)}
    for s in order[::-1]:
        for t in range(wide):
            pieces[s, t] = shifted(column[s], 0, t, 0) if t else column[s]
    mine = jnp.stack([pieces[s, t] for s in range(tall) for t in range(wide)])
    other = shifted(mine, 0, 0, 1)
    return jnp.stack([mine, other], axis=1).reshape(-1, block.shape[-1])


def scattered(partial, rows):
    tall, wide = grid_of(lax.axis_size("mesh"))
    width = partial.shape[-1]
    narrow = jnp.bfloat16
    blocks = partial.reshape(tall, wide, CORES, rows, width)
    came = shifted(blocks[:, :, 1].astype(narrow), 0, 0, -1)
    chip = blocks[:, :, 0] + came.astype(jnp.float32)
    order = sorted(range(1, tall), key=lambda s: -min(s, tall - s)) + [0]
    lines = {}
    total = None
    for s in order:
        line = chip[s, 0]
        for t in range(1, wide):
            line = line + shifted(chip[s, t].astype(narrow), 0, -t, 0).astype(jnp.float32)
        lines[s] = line if s == 0 else shifted(line.astype(narrow), -s, 0, 0).astype(jnp.float32)
    for s in order[::-1]:
        total = lines[s] if total is None else total + lines[s]
    return total


def row_names(micro, tokens_here):
    devices = lax.axis_size("mesh")
    tall, wide = grid_of(devices)
    me = lax.axis_index("mesh")
    z, y, c = me // (CORES * wide), me // CORES % wide, me % CORES
    shape = (tall, wide, CORES, micro, tokens_here)
    at = [lax.broadcasted_iota(jnp.int32, shape, d) for d in range(5)]
    owner = ((z - at[0] + tall) % tall * wide + (y - at[1] + wide) % wide) * CORES + (c - at[2] + CORES) % CORES
    return at[3].reshape(-1), (owner * tokens_here + at[4]).reshape(-1)


def build_mask(micro, tokens_here):
    batch, token = row_names(micro, tokens_here)
    same_batch = batch[:, None] == batch[None, :]
    same_frame = token[:, None] // PATCHES == token[None, :] // PATCHES
    same_patch = token[:, None] % PATCHES == token[None, :] % PATCHES
    parity = lax.axis_index("section") % 2
    return same_batch & jnp.where(parity == 0, same_frame, same_patch)


def section_layer(residual, gain_row, packed_weight, out_rows, attend_mask):
    rows = residual.shape[0]
    stream = gathered(residual.astype(jnp.bfloat16)).astype(jnp.float32)
    mean_square = jnp.mean(stream * stream, axis=-1, keepdims=True)
    normed = (stream * lax.rsqrt(mean_square + epsilon) * gain_row[None, :]).astype(jnp.bfloat16)
    packed = jnp.dot(normed, packed_weight, preferred_element_type=jnp.float32).astype(jnp.bfloat16)
    total_rows = packed.shape[0]
    heads_here = packed.shape[1] // (3 * HEAD_DIM)
    packed = packed.reshape(total_rows, heads_here, 3, HEAD_DIM)
    scores = jnp.einsum(
        "thd,shd->hts", packed[:, :, 0], packed[:, :, 1], preferred_element_type=jnp.float32
    )
    scores = jnp.where(attend_mask[None], scores * HEAD_DIM ** (-0.5), -1e30)
    weights = jax.nn.softmax(scores, axis=-1).astype(jnp.bfloat16)
    attended = jnp.einsum(
        "hts,shd->thd", weights, packed[:, :, 2], preferred_element_type=jnp.float32
    )
    attended = attended.astype(jnp.bfloat16).reshape(total_rows, heads_here * HEAD_DIM)
    partial = jnp.dot(attended, out_rows, preferred_element_type=jnp.float32)
    return residual + scattered(partial, rows)


def per_device(video_tokens, norm_gain, qkv_weight, out_weight):
    section_count = lax.axis_size("section")
    section_index = lax.axis_index("section")
    gain_row = norm_gain[0]
    packed_weight = qkv_weight[0]
    out_rows = out_weight[0]
    micro, tokens_here, width = video_tokens.shape
    attend_mask = build_mask(micro, tokens_here)
    current = video_tokens.reshape(micro * tokens_here, width).astype(jnp.float32)
    for moment in range(section_count):
        produced = section_layer(current, gain_row, packed_weight, out_rows, attend_mask)
        if moment < section_count - 1:
            current = passed_along(produced.astype(jnp.bfloat16), "section", 1).astype(jnp.float32)
    share = width // section_count
    last = section_count - 1
    mine = produced[:, last * share :]
    for s in range(last):
        cut = produced[:, s * share : (s + 1) * share].astype(jnp.bfloat16)
        cut = lax.ppermute(cut, "section", [(last, s)]).astype(jnp.float32)
        mine = jnp.where(section_index == s, cut, mine)
    return mine.reshape(micro, tokens_here, share)


def solution(mesh):
    return jax.shard_map(
        per_device,
        mesh=mesh,
        in_specs=(
            P(None, "mesh", None),
            P("section", None),
            P("section", None, "mesh"),
            P("section", "mesh", None),
        ),
        out_specs=P(None, "mesh", "section"),
        check_vma=False,
    )
```

```python
import functools

import jax
import jax.numpy as jnp
from jax import lax
from jax.experimental import pallas as pl
from jax.experimental.pallas import tpu as pltpu
from jax.sharding import PartitionSpec as P

HEAD_DIM = 96
PATCHES = 64

epsilon = 1e-06
narrow, wide = jnp.bfloat16, jnp.float32


SHORT_BITS = 4


def bits_of(devices):
    return devices.bit_length() - 1


def is_short(devices, sections):
    return bits_of(devices) == SHORT_BITS and sections == 2


def swapped(block, bit):
    devices = lax.axis_size("mesh")
    return lax.ppermute(block, "mesh", [(i, i ^ (1 << bit)) for i in range(devices)])


def crossed(block, source, target, flip):
    devices = lax.axis_size("mesh")
    return lax.ppermute(
        block, ("section", "mesh"), [(source * devices + i, target * devices + (i ^ flip)) for i in range(devices)]
    )


def halved_kernel(x_ref, whole_ref, left_ref, right_ref):
    half = left_ref.shape[-1]
    whole_ref[...] = x_ref[...]
    left_ref[...] = x_ref[:, :half]
    right_ref[...] = x_ref[:, half:]


def halved(block):
    rows, width = block.shape
    return pl.pallas_call(
        halved_kernel,
        out_shape=[jax.ShapeDtypeStruct((rows, w), block.dtype) for w in (width, width // 2, width // 2)],
        compiler_params=pltpu.CompilerParams(vmem_limit_bytes=4 << 20),
        cost_estimate=pl.CostEstimate(flops=1 << 34, bytes_accessed=4 * rows * width, transcendentals=0),
        name="halved",
    )(block)


def gathered(block, lefts):
    bits = bits_of(lax.axis_size("mesh"))
    top = 1 << (bits - 1)
    half = block.shape[-1] // 2
    full = {0: block}
    for bit in range(bits - 2, 0, -1):
        for k in list(full):
            full[k | 1 << bit] = swapped(full[k], bit)
    halves = []
    for f in range(2):
        part = {top: swapped(lefts[f], bits - 1)}
        for bit in range(bits - 2, 0, -1):
            for k in list(part):
                part[k | 1 << bit] = swapped(part[k], bit)
        halves.append(part)
    other = {k: swapped(full[k], 0) for k in full}
    streams = []
    for f in range(2):
        far = {k: swapped(v, 0) for k, v in halves[f].items()}
        lot = []
        for near_part, far_part in ((full, halves[f]), (other, far)):
            lot += [near_part[k][:, f * half : (f + 1) * half] for k in sorted(near_part)]
            lot += [far_part[k] for k in sorted(far_part)]
        streams.append(jnp.concatenate(lot))
    return streams


def chip_sums(attended, out_halves, rows):
    top = lax.axis_size("mesh") // 2
    half = out_halves[0].shape[-1]
    chips = []
    for f in range(2):
        part = jnp.dot(attended, out_halves[f], preferred_element_type=wide).astype(narrow)
        part = part.reshape(2, top, rows, half)
        came = swapped(part[1], 0)
        chip = part[0].astype(wide) + came.astype(wide)
        chips.append({2 * i: chip[i] for i in range(top)})
    return chips


def lines(chips):
    bits = bits_of(lax.axis_size("mesh"))
    top, n = 1 << (bits - 1), 1 << (bits - 2)
    far = []
    for f in range(2):
        line = {}
        for k in (top | n, top):
            came = swapped(chips[f][k | 2].astype(narrow), 1)
            line[k] = chips[f][k] + came.astype(wide)
        came = swapped(line[top | n].astype(narrow), bits - 2)
        far.append(line[top] + came.astype(wide))
    near = {}
    for k in (n, 0):
        came = swapped(jnp.concatenate([chips[f][k | 2] for f in range(2)], -1).astype(narrow), 1)
        near[k] = jnp.concatenate([chips[f][k] for f in range(2)], -1) + came.astype(wide)
    near[n] = near[n].astype(narrow)
    return far, near[n], near[0]


def same_group(rows, micro, tokens_here, axis):
    chips = lax.axis_size("mesh") // 2

    def split(number, size):
        return lax.shift_right_logical(number, size.bit_length() - 1), number & (size - 1)

    row, token = split(lax.broadcasted_iota(jnp.int32, (rows, rows), axis), tokens_here)
    place, batch = split(row, micro)
    core, other = split(place, chips)
    owner = (other * 2 + core) ^ lax.axis_index("mesh")
    frame, patch = split(owner * tokens_here + token, PATCHES)
    parity = lax.axis_index("section") % 2
    return batch + micro * jnp.where(parity == 0, frame, patch)


def attention_kernel(micro, tokens_here, packed_ref, out_ref):
    rows = packed_ref.shape[0]
    heads = packed_ref.shape[1] // (3 * HEAD_DIM)
    allowed = same_group(rows, micro, tokens_here, 0) == same_group(rows, micro, tokens_here, 1)
    for h in range(heads):
        queries, keys, values = [
            packed_ref[:, (3 * h + i) * HEAD_DIM : (3 * h + i + 1) * HEAD_DIM] for i in range(3)
        ]
        scores = lax.dot_general(queries, keys, (((1,), (1,)), ((), ())), preferred_element_type=wide)
        scores = jnp.where(allowed, scores * HEAD_DIM ** (-0.5), -1e30)
        weights = jnp.exp(scores - jnp.max(scores, axis=-1, keepdims=True))
        weights = (weights / jnp.sum(weights, axis=-1, keepdims=True)).astype(narrow)
        part = jnp.dot(weights, values, preferred_element_type=wide)
        out_ref[:, h * HEAD_DIM : (h + 1) * HEAD_DIM] = part.astype(narrow)


def attention(streams, gain_row, packed_halves, micro, tokens_here):
    half = streams[0].shape[-1]
    square = 0.0
    for f, stream in enumerate(streams):
        rows = stream.astype(wide)
        square = square + jnp.sum(rows * rows, axis=-1, keepdims=True)
        scaled = (rows * gain_row[None, f * half : (f + 1) * half]).astype(narrow)
        part = jnp.dot(scaled, packed_halves[f], preferred_element_type=wide)
        packed = part if f == 0 else lax.optimization_barrier(packed) + part
    packed = (packed * lax.rsqrt(square / (2 * half) + epsilon)).astype(narrow)
    total_rows, columns = packed.shape
    return pl.pallas_call(
        functools.partial(attention_kernel, micro, tokens_here),
        out_shape=jax.ShapeDtypeStruct((total_rows, columns // 3), narrow),
        compiler_params=pltpu.CompilerParams(vmem_limit_bytes=8 << 20),
        cost_estimate=pl.CostEstimate(
            flops=4 * total_rows * total_rows * columns // 3,
            bytes_accessed=2 * total_rows * columns,
            transcendentals=total_rows * total_rows * columns // (3 * HEAD_DIM),
        ),
        name="attention",
    )(packed)


def short_program(block, gain_row, packed_weight, out_rows, micro, tokens_here):
    section_index = lax.axis_index("section")
    bits = bits_of(lax.axis_size("mesh"))
    top, n = 1 << (bits - 1), 1 << (bits - 2)
    rows, width = block.shape
    half = width // 2
    block, *lefts = halved(block)
    packed_halves = [packed_weight[:half], packed_weight[half:]]
    out_halves = [out_rows[:, :half], out_rows[:, half:]]
    attended = attention(gathered(block, lefts), gain_row, packed_halves, micro, tokens_here)
    far, beside, own = lines(chip_sums(attended, out_halves, rows))
    came = [crossed(far[f].astype(narrow), 0, 1, top) for f in range(2)]
    stepped = crossed(beside, 0, 1, n)
    straight = crossed((own + block.astype(wide)).astype(narrow), 0, 1, 0)
    residual = straight.astype(wide) + stepped.astype(wide) + jnp.concatenate([c.astype(wide) for c in came], -1)
    block = residual.astype(narrow)
    lefts = [block[:, :half], block[:, half:]]
    attended = attention(gathered(block, lefts), gain_row, packed_halves, micro, tokens_here)
    far, beside, own = lines(chip_sums(attended, out_halves, rows))
    own = own + residual
    total = 0.0
    for f in range(2):
        total = total + crossed(far[f].astype(narrow), 1, f, top).astype(wide)
    for f in range(2):
        part = beside[:, f * half : (f + 1) * half]
        total = total + crossed(part, 1, f, n).astype(wide)
    straight = crossed(own[:, :half].astype(narrow), 1, 0, 0).astype(wide)
    return total + jnp.where(section_index == 1, own[:, half:], straight)


def plain_gathered(block):
    for bit in [*range(1, bits_of(lax.axis_size("mesh"))), 0]:
        block = jnp.concatenate([block, swapped(block, bit)])
    half = block.shape[-1] // 2
    return [block[:, :half], block[:, half:]]


def plain_scattered(chips):
    total = jnp.concatenate([jnp.stack([chip[k] for k in sorted(chip)]) for chip in chips], -1)
    for bit in range(bits_of(lax.axis_size("mesh")) - 1, 0, -1):
        keep, send = jnp.split(total, 2)
        total = keep + swapped(send.astype(narrow), bit).astype(wide)
    return total[0]


def plain_program(block, gain_row, packed_weight, out_rows, micro, tokens_here):
    section_count = lax.axis_size("section")
    section_index = lax.axis_index("section")
    rows, width = block.shape
    last, share = section_count - 1, width // section_count
    current = block.astype(wide)
    packed_halves, out_halves = jnp.split(packed_weight, 2), jnp.split(out_rows, 2, -1)
    for moment in range(section_count):
        attended = attention(plain_gathered(current.astype(narrow)), gain_row, packed_halves, micro, tokens_here)
        current = current + plain_scattered(chip_sums(attended, out_halves, rows))
        if moment < last:
            current = crossed(current.astype(narrow), moment, moment + 1, 0).astype(wide)
    mine = current[:, last * share :]
    for s in range(last):
        cut = crossed(current[:, s * share : (s + 1) * share].astype(narrow), last, s, 0).astype(wide)
        mine = jnp.where(section_index == s, cut, mine)
    return mine


def per_device(video_tokens, norm_gain, qkv_weight, out_weight):
    sections = lax.axis_size("section")
    micro, tokens_here, width = video_tokens.shape
    program = short_program if is_short(lax.axis_size("mesh"), sections) else plain_program
    block = video_tokens.reshape(micro * tokens_here, width)
    mine = program(block, norm_gain[0], qkv_weight[0], out_weight[0], micro, tokens_here)
    return mine.reshape(micro, tokens_here, width // sections)


def solution(mesh):
    return jax.shard_map(
        per_device,
        mesh=mesh,
        in_specs=(
            P(None, "mesh", None),
            P("section", None),
            P("section", None, "mesh"),
            P("section", "mesh", None),
        ),
        out_specs=P(None, "mesh", "section"),
        check_vma=False,
    )
```
